32 devices in a mesh: sec: 4 (over y, x), term: 8 (over z, core).
Axes of the slice: x: 2, y: 2, z: 4, core: 2. Of those that a mesh axis runs over, the one named last changes fastest.
Arguments:
- psi: bfloat16 [32, 384, 384], P('sec'), may hold values from -6 to 6
- left_env: bfloat16 [8, 2, 32, 384, 384], P('term', None, 'sec'), may hold values from -0.3125 to 0.3125
- right_env: bfloat16 [8, 2, 32, 384, 384], P('term', None, 'sec'), may hold values from -0.21875 to 0.21875
- targets: int32 [8, 32], P('term', 'sec'), may hold values from 0 to 31, as said below
- selected: int32 [8, 32], P('term', 'sec'), may hold values from 0 to 1, as said below
- block_dims: int32 [32, 2], P('sec'), may hold values from 192 to 384, as said below
Outputs:
- sigma: bfloat16 [32, 384, 384], P('sec', 'term')
The draws below stay inside these ranges and needn't reach their ends.
Inputs may be any that keep to these rules, and one draw needn't show every extreme that they name: For each term class w, targets[w] is a permutation of the 32 blocks. Blocks k and k2 belong to the same index of sec when k // 8 = k2 // 8; under one term class the blocks of one index of sec go to exactly 4 distinct indices of sec, exactly 2 blocks to each. Under each term class, between 1 and 6 of the 8 blocks of one index of sec are selected, exactly 6 on some index. `block_dims`: some block has both dimensions equal to 384.
All inputs are finite; a program needn't handle non-finite values.
Results may differ from the reference program's by a relative error of at most 0.013.
Values may be sent and summed in bfloat16 or wider, within the bound.
No kernel may reach another device: no remote copies, remote signals or barrier semaphores. Data moves between devices by JAX's collectives and lax.ppermute only.
A program may use at most 64 MiB of HBM per device.

```python
import jax
import jax.numpy as jnp
from jax import lax

BS = 384
COMP = 2
NB_DEV = 8
SEL_DEV = 6
CAP = 2
NB = 32
TERMS = 8


def draw_targets(key, part):
    sec_total = NB // NB_DEV
    groups = min(NB_DEV, sec_total)
    key_off, key_src, key_dst = jax.random.split(key, 3)
    offsets = jax.vmap(lambda one_key: jax.random.permutation(one_key, sec_total)[:groups])(jax.random.split(key_off, TERMS))
    source_perm = jax.vmap(lambda one_key: jax.random.permutation(one_key, NB_DEV))(jax.random.split(key_src, TERMS * sec_total)).reshape(TERMS, sec_total, NB_DEV)
    dest_perm = jax.vmap(lambda one_key: jax.random.permutation(one_key, NB_DEV))(jax.random.split(key_dst, TERMS * sec_total)).reshape(TERMS, sec_total, NB_DEV)
    position = jnp.arange(NB_DEV, dtype=jnp.int32)
    group = position // CAP
    devices = jnp.arange(sec_total, dtype=jnp.int32)
    term_ids = jnp.arange(TERMS, dtype=jnp.int32)
    dest = (devices[None, :, None] + offsets[:, group][:, None, :]) % sec_total
    local_slot = dest_perm[term_ids[:, None, None], dest, position[None, None, :]]
    value = dest * NB_DEV + local_slot
    source_block = devices[None, :, None] * NB_DEV + source_perm
    term_grid = jnp.broadcast_to(term_ids[:, None, None], value.shape)
    result = jnp.zeros((TERMS, NB), jnp.int32).at[term_grid, source_block].set(value.astype(jnp.int32))
    return result.astype(jnp.int32)


def draw_selected(key, part):
    sec_total = NB // NB_DEV
    key_count, key_first, key_perm = jax.random.split(key, 3)
    counts = jax.random.randint(key_count, (TERMS, sec_total), 1, SEL_DEV + 1)
    first = jax.random.randint(key_first, (TERMS,), 0, sec_total)
    counts = jnp.where(jnp.arange(sec_total)[None, :] == first[:, None], SEL_DEV, counts)
    ranks = jax.vmap(lambda one_key: jax.random.permutation(one_key, NB_DEV))(jax.random.split(key_perm, TERMS * sec_total)).reshape(TERMS, sec_total, NB_DEV)
    chosen = (ranks < counts[:, :, None]).astype(jnp.int32)
    return chosen.reshape(TERMS, NB)


def draw_block_dims(key, part):
    key_dims, key_full = jax.random.split(key, 2)
    dims = jax.random.randint(key_dims, (NB, 2), BS // 2, BS + 1)
    full = jax.random.randint(key_full, (), 0, NB)
    dims = jnp.where(jnp.arange(NB)[:, None] == full, BS, dims)
    return dims.astype(jnp.int32)


def steps_of(rng, shape, cuts, smallest, top_value):
    factor_of = 1.0
    for dim, shards_of in cuts:
        steps = jax.random.uniform(jax.random.fold_in(jax.random.fold_in(rng, 6), dim), (shards_of,), jnp.float32, smallest / len(cuts), top_value / len(cuts))
        factor_of = factor_of * jnp.repeat(jnp.exp(steps), shape[dim] // shards_of).reshape((-1,) + (1,) * (len(shape) - 1 - dim))
    return factor_of


def normal_values(key, shape, scale, limit, cuts=(), kind=jnp.bfloat16):
    entries = jax.random.normal(key, shape, jnp.float32) * scale
    if len(cuts) > 0:
        entries = steps_of(key, shape, cuts, -0.22, 0.18) * entries
    return jnp.clip(entries, min=-limit, max=limit).astype(kind)


def setup_inputs(seed: int = 0) -> dict:
    splits = jax.random.split(jax.random.key(seed), 7)
    psi = normal_values(splits[0], (NB, BS, BS), 1.0, 6.0, ((0, 4),))
    left_env = normal_values(splits[1], (TERMS, COMP, NB, BS, BS), BS ** -0.5, 0.3125, ((0, 8), (2, 4)))
    right_env = normal_values(splits[2], (TERMS, COMP, NB, BS, BS), (COMP * BS) ** -0.5, 0.21875, ((0, 8), (2, 4)))
    targets = draw_targets(jax.random.fold_in(splits[6], 71), 0)
    selected = draw_selected(jax.random.fold_in(splits[6], 71), 0)
    block_dims = draw_block_dims(jax.random.fold_in(splits[6], 71), 0)
    return dict(psi=psi, left_env=left_env, right_env=right_env, targets=targets, selected=selected, block_dims=block_dims)


def reference(psi, left_env, right_env, targets, selected, block_dims):
    positions = jnp.arange(BS, dtype=jnp.int32)
    rows_ok = positions[None, :] < block_dims[:, 0:1]
    cols_ok = positions[None, :] < block_dims[:, 1:2]
    inside = rows_ok[:, :, None] & cols_ok[:, None, :]
    masked = jnp.where(inside, psi, jnp.zeros_like(psi))

    def one_term(summed, term_inputs):
        left_now, right_now, target, chosen = term_inputs
        half_product = jnp.einsum("mkab,kbc->mkac", left_now.astype(jnp.float32), masked.astype(jnp.float32)).astype(jnp.bfloat16)
        term_block = jnp.einsum("mkab,mkbc->kac", half_product.astype(jnp.float32), right_now.astype(jnp.float32))
        term_block = (term_block * chosen.astype(jnp.float32)[:, None, None]).astype(jnp.bfloat16)
        summed = summed.at[target.astype(jnp.int32)].add(term_block.astype(jnp.float32))
        return summed, None

    start = jnp.zeros((NB, BS, BS), jnp.float32)
    summed, unused = lax.scan(one_term, start, (left_env, right_env, targets, selected))
    return jnp.where(inside, summed, jnp.zeros_like(summed)).astype(jnp.bfloat16)
```

```python
import functools

import jax
import jax.numpy as jnp
from jax import lax
from jax.experimental import pallas as pl
from jax.experimental.pallas import tpu as pltpu
from jax.sharding import PartitionSpec as P

LANES = 128


def ring(sec_count, term_count, sec_step, term_step):
    return [
        (s * term_count + w, (s ^ sec_step) * term_count + (w ^ term_step))
        for s in range(sec_count)
        for w in range(term_count)
    ]


def product_kernel(
    place, targets, chosen, dims, psi, left, right, *rest, sec_count, cap, z_count, tile, chunks, width
):
    message_count = sec_count * 2 * chunks
    messages = rest[:message_count]
    left_v, right_v, psi_v, half_v, out_v, source, in_sems, out_sems = rest[message_count:]
    blocks = psi.shape[0]
    size = psi.shape[1]
    slots = sec_count * cap
    parts = z_count * (size // (2 * z_count * tile))
    sec_here = place[0]
    core_here = place[1]

    def clear(slot, carry):
        source[0, slot] = -1
        return carry

    lax.fori_loop(0, slots, clear, 0)
    for q in range(sec_count):
        source[1, q] = 0

    def locate(k, carry):
        q = (targets[0, k] // blocks) ^ sec_here
        rank = source[1, q]
        source[1, q] = rank + 1
        source[0, q * cap + rank] = k
        return carry

    lax.fori_loop(0, blocks, locate, 0)

    def copies(k):
        return (
            pltpu.make_async_copy(left.at[0, :, k], left_v.at[k], in_sems.at[0, k]),
            pltpu.make_async_copy(right.at[0, :, k], right_v.at[k], in_sems.at[1, k]),
            pltpu.make_async_copy(psi.at[k], psi_v.at[k], in_sems.at[2, k]),
        )

    def sends(q):
        for e in range(2):
            for c in range(chunks):
                rows = messages[(q * 2 + e) * chunks + c].shape[0]
                yield pltpu.make_async_copy(
                    out_v.at[q, e, pl.ds(0, rows), :, pl.ds(c * width, width)],
                    messages[(q * 2 + e) * chunks + c],
                    out_sems.at[q, e, c],
                )

    def fetch(i, carry):
        k = source[0, slots - 1 - i]
        known = jnp.maximum(k, 0)

        @pl.when((k >= 0) & (chosen[0, known] > 0))
        def _():
            for copy in copies(known):
                copy.start()

        return carry

    lax.fori_loop(0, slots, fetch, 0)

    def compute(i, carry):
        slot = slots - 1 - i
        q = slot // cap
        rank = slot % cap
        k = source[0, slot]
        known = jnp.maximum(k, 0)
        active = (k >= 0) & (chosen[0, known] > 0)
        first = pl.multiple_of(rank * parts, parts)

        @pl.when(active)
        def _():
            for copy in copies(known):
                copy.wait()
            row = lax.broadcasted_iota(jnp.int32, (size, size), 0)
            col = lax.broadcasted_iota(jnp.int32, (size, size), 1)
            inside = (row < dims[0, known]) & (col < dims[1, known])
            masked = jnp.where(inside, psi_v[known].astype(jnp.float32), 0.0).astype(jnp.bfloat16)
            comps = left_v.shape[1]
            half = jnp.dot(
                left_v[known].reshape(comps * size, size), masked, preferred_element_type=jnp.float32
            ).astype(jnp.bfloat16)
            for m in range(comps):
                half_v[:, m * size : (m + 1) * size] = half[m * size : (m + 1) * size]
            result = jnp.dot(
                half_v[...],
                right_v[known].reshape(comps * size, size),
                preferred_element_type=jnp.float32,
            )
            split = result.reshape(z_count, 2, parts // z_count, tile, size).astype(jnp.bfloat16)
            for core in range(2):
                out_v[q, core ^ core_here, pl.ds(first, parts)] = split[:, core].reshape(
                    parts, tile, size
                )

        @pl.when(jnp.logical_not(active))
        def _():
            for e in range(2):
                out_v[q, e, pl.ds(first, parts)] = jnp.zeros((parts, tile, size), jnp.bfloat16)

        for q_now in range(sec_count):

            @pl.when(slot == q_now * cap)
            def _(q_now=q_now):
                row = lax.broadcasted_iota(jnp.int32, (tile, size), 0)
                mark = jnp.zeros((tile, size), jnp.float32)
                for r in range(cap):
                    block = source[0, q_now * cap + r]
                    local = targets[0, jnp.maximum(block, 0)] % blocks
                    ident = jnp.where(block >= 0, local + 1, 0).astype(jnp.float32)
                    mark = jnp.where(row == r, ident, mark)
                for e in range(2):
                    out_v[q_now, e, cap * parts] = mark.astype(jnp.bfloat16)
                for copy in sends(q_now):
                    copy.start()

        return carry

    lax.fori_loop(0, slots, compute, 0)
    for q in range(sec_count):
        for copy in sends(q):
            copy.wait()


def merge_kernel(place, *refs, sec_count, cap, z_count, first_chunk):
    message_count = sec_count * 2
    if first_chunk:
        messages = refs[:message_count]
        outs = refs[message_count : message_count + z_count]
        where, arrived, sems = refs[message_count + z_count :]
    else:
        where = refs[0]
        messages = refs[1 : 1 + message_count]
        outs = refs[1 + message_count : 1 + message_count + z_count]
        arrived, sems = refs[1 + message_count + z_count :]
    blocks, parts_z, tile, width = outs[0].shape
    parts = parts_z * z_count
    z_here = place[2]
    copies = [
        pltpu.make_async_copy(messages[i], arrived.at[i % 2, i // 2], sems.at[i])
        for i in range(message_count)
    ]
    for copy in copies:
        copy.start()
    for copy in copies:
        copy.wait()
    if first_chunk:
        for e in range(2):
            for q in range(sec_count):
                mark = arrived[e, q, cap * parts].astype(jnp.float32)
                for r in range(cap):
                    ident = jnp.max(mark[r : r + 1]).astype(jnp.int32)

                    @pl.when(ident > 0)
                    def _(e=e, q=q, r=r, ident=ident):
                        where[e, ident - 1] = q * cap + r

    def add(j, carry):
        here = where[0, j]
        there = where[1, j]
        for dz in range(z_count):
            start = (z_here ^ dz) * parts_z
            a = arrived[0, here // cap, pl.ds((here % cap) * parts + start, parts_z)]
            b = arrived[1, there // cap, pl.ds((there % cap) * parts + start, parts_z)]
            outs[dz][j] = (a.astype(jnp.float32) + b.astype(jnp.float32)).astype(jnp.bfloat16)
        return carry

    lax.fori_loop(0, blocks, add, 0)


def final_kernel(place, dims, *refs, z_count, chunks):
    out = refs[-1]
    blocks, rows, size = out.shape
    _, parts_z, tile, width = refs[0].shape
    row_first = place[3] * rows

    def one(j, carry):
        for c in range(chunks):
            total = refs[c * z_count][j].astype(jnp.float32)
            for dz in range(1, z_count):
                total = total + refs[c * z_count + dz][j].astype(jnp.float32)
            total = total.reshape(rows, width)
            row = lax.broadcasted_iota(jnp.int32, (rows, width), 0) + row_first
            col = lax.broadcasted_iota(jnp.int32, (rows, width), 1) + c * width
            keep = (row < dims[0, j]) & (col < dims[1, j])
            out[j, :, c * width : (c + 1) * width] = jnp.where(keep, total, 0.0).astype(jnp.bfloat16)
        return carry

    lax.fori_loop(0, blocks, one, 0)


def shards(psi, left_env, right_env, targets, selected, block_dims):
    sec_count = lax.axis_size("sec")
    term_count = lax.axis_size("term")
    blocks, size, _ = psi.shape
    comps = left_env.shape[1]
    cap = blocks // min(blocks, sec_count)
    slots = sec_count * cap
    z_count = term_count // 2
    rows = size // term_count
    tile = 16 if rows % 16 == 0 else 8
    width = LANES if size % LANES == 0 else size
    chunks = size // width
    parts_z = rows // tile
    parts = parts_z * z_count
    sec_here = lax.axis_index("sec")
    term_here = lax.axis_index("term")
    place = jnp.stack([sec_here, term_here % 2, term_here // 2, term_here]).astype(jnp.int32)
    dims = block_dims.T
    smem = pl.BlockSpec(memory_space=pltpu.SMEM)
    vmem = pl.BlockSpec(memory_space=pltpu.VMEM)
    anywhere = pl.BlockSpec(memory_space=pl.ANY)
    axes = ("sec", "term")

    def message(c):
        return jax.ShapeDtypeStruct((cap * parts + (c == 0), tile, width), jnp.bfloat16)

    messages = pl.pallas_call(
        functools.partial(
            product_kernel,
            sec_count=sec_count,
            cap=cap,
            z_count=z_count,
            tile=tile,
            chunks=chunks,
            width=width,
        ),
        out_shape=[message(c) for q in range(sec_count) for e in range(2) for c in range(chunks)],
        in_specs=[smem] * 4 + [anywhere] * 3,
        out_specs=[anywhere] * (sec_count * 2 * chunks),
        scratch_shapes=[
            pltpu.VMEM((blocks, comps, size, size), jnp.bfloat16),
            pltpu.VMEM((blocks, comps, size, size), jnp.bfloat16),
            pltpu.VMEM((blocks, size, size), jnp.bfloat16),
            pltpu.VMEM((size, comps * size), jnp.bfloat16),
            pltpu.VMEM((sec_count, 2, cap * parts + 1, tile, size), jnp.bfloat16),
            pltpu.SMEM((2, slots), jnp.int32),
            pltpu.SemaphoreType.DMA((3, blocks)),
            pltpu.SemaphoreType.DMA((sec_count, 2, chunks)),
        ],
        compiler_params=pltpu.CompilerParams(vmem_limit_bytes=60000 * 1024),
        name="products",
    )(place, targets, selected, dims, psi, left_env, right_env)

    where = None
    pieces = []
    for c in range(chunks):
        arrived = [None] * (sec_count * 2)
        for q in reversed(range(sec_count)):
            for e in range(2):
                sent = messages[(q * 2 + e) * chunks + c]
                if q or e:
                    sent = lax.ppermute(sent, axes, ring(sec_count, term_count, q, e))
                arrived[q * 2 + e] = sent
        piece = jax.ShapeDtypeStruct((blocks, parts_z, tile, width), jnp.bfloat16)
        outs = [piece] * z_count
        out_specs = [vmem] * z_count
        if c == 0:
            outs = outs + [jax.ShapeDtypeStruct((2, blocks), jnp.int32)]
            out_specs = out_specs + [smem]
        merged = pl.pallas_call(
            functools.partial(
                merge_kernel, sec_count=sec_count, cap=cap, z_count=z_count, first_chunk=c == 0
            ),
            out_shape=outs,
            in_specs=[smem] * (1 + (c > 0)) + [anywhere] * (sec_count * 2),
            out_specs=out_specs,
            scratch_shapes=[
                pltpu.VMEM((2, sec_count) + message(c).shape, jnp.bfloat16),
                pltpu.SemaphoreType.DMA((sec_count * 2,)),
            ],
            name=f"merge_{c}",
        )(place, *([] if c == 0 else [where]), *arrived)
        if c == 0:
            where = merged[z_count]
        pieces.append(merged[0])
        for dz in range(1, z_count):
            pieces.append(lax.ppermute(merged[dz], axes, ring(sec_count, term_count, 0, 2 * dz)))

    return pl.pallas_call(
        functools.partial(final_kernel, z_count=z_count, chunks=chunks),
        out_shape=jax.ShapeDtypeStruct((blocks, rows, size), jnp.bfloat16),
        in_specs=[smem] * 2 + [vmem] * len(pieces),
        out_specs=vmem,
        name="finish",
    )(place, dims, *pieces)


def solution(mesh):
    return jax.shard_map(
        shards,
        mesh=mesh,
        in_specs=(
            P("sec", None, None),
            P("term", None, "sec", None, None),
            P("term", None, "sec", None, None),
            P("term", "sec"),
            P("term", "sec"),
            P("sec", None),
        ),
        out_specs=P("sec", "term", None),
        check_vma=False,
    )
```
